32 devices in a mesh: row: 16 (over z, y, x), col: 2 (over core).
Axes of the slice: x: 2, y: 2, z: 4, core: 2. Of those that a mesh axis runs over, the one named last changes fastest.
Arguments:
- acts: bfloat16 [2048, 8192], P('row'), may hold values from -22 to 22
- out_grads: bfloat16 [2048, 4096], P('row', 'col'), may hold values from -0.198873782 to 0.198873782
- weight: float32 [8192, 4096], P('row', 'col'), may hold values from -30 to 30
- row_state: float32 [8192], P('row'), may hold values from 0.002 to 2
- col_state: float32 [4096], P('col'), may hold values from 0.01 to 0.3
Outputs:
- new_weight: float32 [8192, 4096], P('row', 'col')
- update: float32 [8192, 4096], P('row', 'col')
- row_moment: float32 [8192], P('row')
- col_moment: float32 [4096], P('col')
The draws below stay inside these ranges and needn't reach their ends.
All inputs are finite; a program needn't handle non-finite values.
Results may differ from the reference program's by a relative error of at most 0.0003.
Values may be sent and summed in bfloat16 or wider, within the bound.
No kernel may reach another device: no remote copies, remote signals or barrier semaphores. Data moves between devices by JAX's collectives and lax.ppermute only.
A program may use at most 64 MiB of HBM per device.

```python
import math
import jax
import jax.numpy as jnp
from jax import lax

D = 8192
HEAD_DIM = 256
HEADS = 16
FW = 4096
TOKENS = 2048


def row_ramp(count, top):
    frac = jnp.arange(count, dtype=jnp.float32) / jnp.float32(max(count - 1, 1))
    return jnp.exp(jnp.log(jnp.float32(top)) * frac)


def group_factor(count):
    tok_first = (jnp.arange(TOKENS) < TOKENS // 2)[:, None]
    feat_first = (jnp.arange(count) < count // 2)[None, :]
    return jnp.where(jnp.logical_and(tok_first, feat_first), 1.5, 0.5).astype(jnp.float32)


def draw_acts(key, part):
    inner = jax.random.fold_in(key, 11)
    values = jnp.clip(jax.random.normal(inner, (TOKENS, D), jnp.float32), -6.0, 6.0)
    values = values * jnp.sqrt(row_ramp(D, 30.0))[None, :]
    values = values * group_factor(D)
    return values.astype(jnp.bfloat16)


def draw_out_grads(key, part):
    inner = jax.random.fold_in(key, 23)
    scale = 1.0 / jnp.sqrt(jnp.float32(TOKENS))
    values = jnp.clip(jax.random.normal(inner, (TOKENS, FW), jnp.float32), -6.0, 6.0)
    values = values * group_factor(FW)
    return (values * scale).astype(jnp.bfloat16)


def column_factor(key):
    head_key = jax.random.fold_in(key, 53)
    head_scale = jnp.exp(jax.random.uniform(head_key, (HEADS,), jnp.float32, -1.2, 0.0))
    per_column = jnp.repeat(head_scale, HEAD_DIM)
    frac = jnp.arange(FW, dtype=jnp.float32) / jnp.float32(max(FW - 1, 1))
    return per_column * jnp.exp(-0.8 * frac)


def draw_weight(key, part):
    inner = jax.random.fold_in(key, 37)
    values = jnp.clip(jax.random.normal(inner, (D, FW), jnp.float32), -3.0, 3.0)
    values = values * row_ramp(D, 10.0)[:, None]
    return values * column_factor(key)[None, :]


def draw_row_state(key, part):
    inner = jax.random.fold_in(key, 41)
    noise = jnp.exp(jax.random.uniform(inner, (D,), jnp.float32, -0.6931472, 0.6931472))
    values = 0.5 * row_ramp(D, 0.02) * noise
    return values


def steps_of(stream_key, dims, cuts, least, high):
    level = 1.0
    for axis_at, shards_of in cuts:
        draws = jax.random.uniform(jax.random.fold_in(jax.random.fold_in(stream_key, 6), axis_at), (shards_of,), jnp.float32, least / len(cuts), high / len(cuts))
        level = level * jnp.repeat(jnp.exp(draws), dims[axis_at] // shards_of).reshape((-1,) + (1,) * (len(dims) - 1 - axis_at))
    return level


def setup_inputs(seed: int = 0) -> dict:
    splits = jax.random.split(jax.random.key(seed), 6)
    return {
        "acts": draw_acts(jax.random.fold_in(splits[5], 71), 0),
        "out_grads": draw_out_grads(jax.random.fold_in(splits[5], 71), 0),
        "weight": draw_weight(jax.random.fold_in(splits[5], 71), 0),
        "row_state": draw_row_state(jax.random.fold_in(splits[5], 71), 0),
        "col_state": jnp.clip(jnp.exp(math.log(0.3) - 3.4011974 * jax.random.uniform(splits[4], (FW,), jnp.float32) ** steps_of(splits[4], (FW,), ((0, 2),), -0.2, 0.2)), 0.01, 0.3),
    }


decay_rate = 0.85
floor_eps = 1e-30
relative_rate = 0.05

def reference(acts, out_grads, weight, row_state, col_state):
    gradient = lax.dot_general(acts, out_grads, (((0,), (0,)), ((), ())), preferred_element_type=jnp.float32)
    squares = gradient * gradient + floor_eps
    row_moment = decay_rate * row_state + (1.0 - decay_rate) * lax.optimization_barrier(jnp.mean(squares, axis=1))
    col_moment = decay_rate * col_state + (1.0 - decay_rate) * lax.optimization_barrier(jnp.mean(squares, axis=0))
    unclipped = gradient * lax.rsqrt(row_moment[:, None] * col_moment[None, :])
    clip_factor = jnp.maximum(1.0, jnp.sqrt(jnp.mean(unclipped * unclipped)))
    update = unclipped / clip_factor
    step_size = relative_rate * jnp.sqrt(jnp.mean(weight * weight) + 1e-06)
    new_weight = weight - step_size * update
    return (new_weight, update, row_moment, col_moment)
```

```python
import jax
import jax.numpy as jnp
from jax import lax
from jax.sharding import PartitionSpec as P

decay_rate = 0.85
floor_eps = 1e-30
relative_rate = 0.05


def butterfly(value, axis, offsets):
    n = lax.axis_size(axis)
    terms = [value]
    for offset in offsets:
        terms = terms + [
            lax.ppermute(value, axis, [(i, i ^ (offset ^ seen)) for i in range(n)])
            for seen in spans(offsets[: offsets.index(offset)])
        ]
    while len(terms) > 1:
        terms = [a + b for a, b in zip(terms[::2], terms[1::2])]
    return terms[0]


def spans(offsets):
    out = [0]
    for offset in offsets:
        out = out + [offset ^ s for s in out]
    return out


def powers(first, end):
    out = []
    while first < end:
        out.append(first)
        first *= 2
    return out


def per_device(acts, out_grads, weight, row_state, col_state):
    n_row = lax.axis_size("row")
    n_col = lax.axis_size("col")
    depth = n_row // 4
    width = acts.shape[1]
    rows_here = width // n_row
    tokens = acts.shape[0]
    half = tokens // 2
    cols_here = out_grads.shape[1]
    cols_all = cols_here * n_col
    me = lax.axis_index("row")
    side = lax.axis_index("col") % 2

    def swap_x(v, name):
        with jax.named_scope(name):
            return lax.ppermute(v, "row", [(i, i ^ 1) for i in range(n_row)])

    def swap_y(v, name):
        with jax.named_scope(name):
            return lax.ppermute(v, "row", [(i, i ^ 2) for i in range(n_row)])

    def next_z(v, name):
        with jax.named_scope(name):
            return lax.ppermute(v, "row", [(i, (i + 4) % n_row) for i in range(n_row)])

    def other_side(v):
        return lax.ppermute(v, "col", [(i, i ^ 1) for i in range(n_col)])

    own = out_grads
    by_x = swap_x(own, "x0")
    by_y = swap_y(own, "y0")
    own_z = next_z(own, "z1")
    mine = lax.dynamic_slice_in_dim(acts, side * half, half, 0)
    blocks = mine.reshape(half, n_row, rows_here).transpose(1, 0, 2)
    mine = lax.all_to_all(blocks, "row", 0, 0, tiled=True)

    top = swap_y(by_x[:half], "dy0")
    low = swap_x(by_y[half:], "dx0")
    pieces = [own, by_x, by_y, top, low]
    quarter = half // 2
    for k in range(1, depth):
        own = own_z
        by_x = swap_x(own, f"x{k}")
        by_y = swap_y(own, f"y{k}")
        if k + 1 < depth:
            own_z = next_z(own, f"z{k + 1}")
        top = next_z(top, f"e{k}")
        q1 = swap_y(by_x[half : half + quarter], f"dy{k}")
        q2 = swap_x(by_y[half + quarter :], f"dx{k}")
        pieces += [own, by_x, by_y, top, q1, q2]
    others = other_side(mine)
    both = jnp.where(side == 0, jnp.stack([mine, others], 1), jnp.stack([others, mine], 1))
    at = jnp.array([((-k % depth) * 4) for k in range(depth)], jnp.int32)
    plane = ((me // 4) * 4 + at) % n_row
    index = plane[:, None] + ((me % 4) ^ jnp.arange(4, dtype=jnp.int32))[None, :]
    columns = jnp.take(both.reshape(n_row, tokens, rows_here), index.reshape(-1), axis=0)
    gradient = lax.dot_general(
        columns.reshape(n_row * tokens, rows_here),
        jnp.concatenate(pieces, 0),
        (((0,), (0,)), ((), ())),
        preferred_element_type=jnp.float32,
    )
    squares = gradient * gradient + floor_eps
    row_total = butterfly(jnp.sum(squares, axis=1), "col", powers(1, n_col))
    row_moment = decay_rate * row_state + (1.0 - decay_rate) * (row_total / cols_all)
    parts = jnp.stack(
        [
            jnp.sum(squares, axis=0),
            jnp.sum(gradient * gradient * (1.0 / row_moment)[:, None], axis=0),
            jnp.sum(weight * weight, axis=0),
        ]
    )
    totals = butterfly(butterfly(parts, "row", [1, 2]), "row", powers(4, n_row))
    col_moment = decay_rate * col_state + (1.0 - decay_rate) * (totals[0] / width)
    sums = jnp.stack([jnp.sum(totals[1] / col_moment), jnp.sum(totals[2])])
    sums = butterfly(sums, "col", powers(1, n_col))
    count_all = width * cols_all
    clip_factor = jnp.maximum(1.0, jnp.sqrt(sums[0] / count_all))
    step_size = relative_rate * jnp.sqrt(sums[1] / count_all + 1e-06)
    update = gradient * lax.rsqrt(row_moment[:, None] * col_moment[None, :]) / clip_factor
    new_weight = weight - step_size * update
    return (new_weight, update, row_moment, col_moment)


def solution(mesh):
    return jax.shard_map(
        per_device,
        mesh=mesh,
        in_specs=(P("row", None), P("row", "col"), P("row", "col"), P("row"), P("col")),
        out_specs=(P("row", "col"), P("row", "col"), P("row"), P("col")),
        check_vma=False,
    )
```

```python
import functools

import jax
import jax.numpy as jnp
from jax import lax
from jax.experimental import pallas as pl
from jax.experimental.pallas import tpu as pltpu
from jax.sharding import PartitionSpec as P

decay_rate = 0.85
floor_eps = 1e-30
relative_rate = 0.05
LANES = 128


def spans(offsets):
    out = [0]
    for offset in offsets:
        out = out + [offset ^ s for s in out]
    return out


def butterfly(value, axis, offsets):
    n = lax.axis_size(axis)
    terms = [value] + [lax.ppermute(value, axis, [(i, i ^ s) for i in range(n)]) for s in spans(offsets)[1:]]
    while len(terms) > 1:
        terms = [a + b for a, b in zip(terms[::2], terms[1::2])]
    return terms[0]


def powers(first, end):
    out = []
    while first < end:
        out.append(first)
        first *= 2
    return out


def placed(space, arrays):
    return [pltpu.with_memory_space_constraint(a, space) for a in arrays]


def in_vmem(*arrays):
    return placed(pltpu.VMEM, arrays)


WHOLE = pl.BlockSpec(memory_space=pltpu.VMEM)
SCALARS = pl.BlockSpec(memory_space=pltpu.SMEM)


def pack_kernel(side_ref, acts_ref, out_ref):
    _, _, width = out_ref.shape
    low = side_ref[0] == 0
    for d in range(out_ref.shape[0]):
        at = 2 * d * width
        a, b = acts_ref[:, at : at + width], acts_ref[:, at + width : at + 2 * width]
        out_ref[d] = jnp.where(low, a, b)


def pack(side, acts, n_row):
    tokens, width = acts.shape
    return pl.pallas_call(
        pack_kernel,
        out_shape=jax.ShapeDtypeStruct((n_row, tokens, width // (2 * n_row)), acts.dtype),
        in_specs=[SCALARS, WHOLE],
        out_specs=WHOLE,
        compiler_params=pltpu.CompilerParams(vmem_limit_bytes=12 << 20),
        cost_estimate=pl.CostEstimate(flops=0, bytes_accessed=3 * acts.size, transcendentals=0),
        name="pack",
    )(side, acts)


def arrange_kernel(index_ref, blocks_ref, out_ref):
    n_row, tokens, _ = blocks_ref.shape
    for s in range(n_row):
        out_ref[:, s * tokens : (s + 1) * tokens] = blocks_ref[index_ref[s]].T


def arrange(index, blocks):
    n_row, tokens, rows = blocks.shape
    return pl.pallas_call(
        arrange_kernel,
        out_shape=pltpu.VMEM((rows, n_row * tokens), blocks.dtype),
        in_specs=[SCALARS, WHOLE],
        out_specs=WHOLE,
        compiler_params=pltpu.CompilerParams(vmem_limit_bytes=12 << 20),
        cost_estimate=pl.CostEstimate(flops=0, bytes_accessed=8 * blocks.size, transcendentals=0),
        name="arrange",
    )(index, *in_vmem(blocks))


def fill(slab, pieces, lanes):
    at = 0
    for piece in pieces:
        slab[at : at + piece.shape[0], :] = piece[:, lanes]
        at += piece.shape[0]


def gemm_kernel(side_ref, mine_ref, other_ref, *refs):
    *pieces, out_ref, slab = refs
    depth = slab.shape[0]
    height = mine_ref.shape[0]
    fill(slab, pieces, slice(None))
    for at, columns_ref in ((side_ref[0], mine_ref), (1 - side_ref[0], other_ref)):
        rows = pl.ds(pl.multiple_of(at * height, height), height)
        out_ref[rows, :] = jnp.dot(columns_ref[:, :depth], slab[...], preferred_element_type=jnp.float32)


def gemm(side, mine, other, pieces):
    rows = 2 * mine.shape[0]
    depth = sum(p.shape[0] for p in pieces)
    cols = pieces[0].shape[1]
    width = min(512, cols)
    return pl.pallas_call(
        gemm_kernel,
        grid=(cols // width,),
        out_shape=jax.ShapeDtypeStruct((rows, cols), jnp.float32),
        in_specs=[SCALARS, WHOLE, WHOLE] + [pl.BlockSpec((p.shape[0], width), lambda j: (0, j)) for p in pieces],
        out_specs=pl.BlockSpec((rows, width), lambda j: (0, j)),
        scratch_shapes=[pltpu.VMEM((depth, width), jnp.bfloat16)],
        compiler_params=pltpu.CompilerParams(vmem_limit_bytes=24 << 20),
        cost_estimate=pl.CostEstimate(flops=2 * rows * depth * cols, bytes_accessed=2 * depth * cols, transcendentals=0),
        name="gemm",
    )(side, *in_vmem(mine, other), *placed(pltpu.HBM, pieces))


def last_kernel(side_ref, mine_ref, other_ref, before_ref, *refs):
    *pieces, out_ref, rows_ref, slab, sums = refs
    depth, width = slab.shape
    height = mine_ref.shape[0]
    first = mine_ref.shape[1] - depth
    cols = out_ref.shape[1]
    side = side_ref[0]
    for t in range(0, cols, width):
        lanes = slice(t, t + width)
        fill(slab, pieces, lanes)
        for at, columns_ref in ((side, mine_ref), (1 - side, other_ref)):
            rows = pl.ds(pl.multiple_of(at * height, height), height)
            total = before_ref[rows, lanes] + jnp.dot(
                columns_ref[:, first:], slab[...], preferred_element_type=jnp.float32
            )
            out_ref[rows, lanes] = total
            squares = total * total + floor_eps
            part = squares[:, :LANES]
            for u in range(LANES, width, LANES):
                part = part + squares[:, u : u + LANES]
            sums[rows, :] = part if t == 0 else sums[rows, :] + part
    rows_ref[...] = jnp.sum(sums[...].T, axis=0, keepdims=True)


def last_gemm(side, mine, other, before, pieces):
    rows, cols = before.shape
    depth = sum(p.shape[0] for p in pieces)
    return pl.pallas_call(
        last_kernel,
        out_shape=[pltpu.VMEM((rows, cols), jnp.float32), pltpu.VMEM((1, rows), jnp.float32)],
        in_specs=[SCALARS] + [WHOLE] * (3 + len(pieces)),
        out_specs=[WHOLE, WHOLE],
        scratch_shapes=[pltpu.VMEM((depth, min(512, cols)), jnp.bfloat16), pltpu.VMEM((rows, LANES), jnp.float32)],
        compiler_params=pltpu.CompilerParams(vmem_limit_bytes=24 << 20),
        cost_estimate=pl.CostEstimate(flops=2 * rows * depth * cols, bytes_accessed=2 * depth * cols, transcendentals=0),
        name="last_gemm",
    )(side, *in_vmem(mine, other, before), *pieces)


def moments_kernel(height, totals_ref, state_ref, col_ref, sums_ref):
    col = decay_rate * state_ref[...] + (1.0 - decay_rate) * (totals_ref[0:1, :] / height)
    col_ref[...] = col
    clip = jnp.sum(totals_ref[1:2, :] / col)
    weight = jnp.sum(totals_ref[2:3, :])
    row = lax.broadcasted_iota(jnp.int32, sums_ref.shape, 0)
    sums_ref[...] = jnp.where(row == 0, clip, weight)


def moments(height, totals, col_state):
    cols = col_state.shape[0]
    whole = pl.BlockSpec(memory_space=pltpu.VMEM)
    return pl.pallas_call(
        functools.partial(moments_kernel, height),
        out_shape=[pltpu.VMEM((1, cols), jnp.float32), pltpu.VMEM((8, LANES), jnp.float32)],
        in_specs=[whole, whole],
        out_specs=[whole, whole],
        compiler_params=pltpu.CompilerParams(vmem_limit_bytes=8 << 20),
        name="moments",
    )(totals, col_state[None, :])


def finish_kernel(count_all, sums_ref, row_ref, col_ref, gradient_ref, weight_ref, new_hbm, update_hbm, new, update, rows, cols, sems):
    clip = jnp.maximum(1.0, jnp.sqrt(sums_ref[0:1, :] / count_all))
    step_size = relative_rate * jnp.sqrt(sums_ref[1:2, :] / count_all + 1e-06)
    root = lax.rsqrt(row_ref[...])
    rows[...] = jnp.broadcast_to(root, (LANES, root.shape[1])).T
    for t in range(0, cols.shape[1], LANES):
        cols[:, t : t + LANES] = lax.rsqrt(col_ref[:, t : t + LANES]) / clip
    height = min(64, rows.shape[0])
    copies = []
    for i in range(rows.shape[0] // height):
        here = slice(i * height, (i + 1) * height)
        scale = rows[here, :]
        for t in range(0, cols.shape[1], LANES):
            lanes = slice(t, t + LANES)
            value = gradient_ref[here, lanes] * scale * cols[:, lanes]
            update[here, lanes] = value
            new[here, lanes] = weight_ref[here, lanes] - step_size * value
        for j, (source, target) in enumerate(((update, update_hbm), (new, new_hbm))):
            copies.append(pltpu.make_async_copy(source.at[here], target.at[here], sems.at[2 * i + j]))
            copies[-1].start()
    for copy in copies:
        copy.wait()


def finish(count_all, sums, row_moment, col_moment, gradient, weight):
    rows, cols = gradient.shape
    out = pltpu.HBM((rows, cols), jnp.float32)
    there = pl.BlockSpec(memory_space=pl.ANY)
    return pl.pallas_call(
        functools.partial(finish_kernel, count_all),
        out_shape=[out, out],
        in_specs=[WHOLE] * 5,
        out_specs=[there, there],
        scratch_shapes=[
            pltpu.VMEM((rows, cols), jnp.float32),
            pltpu.VMEM((rows, cols), jnp.float32),
            pltpu.VMEM((rows, LANES), jnp.float32),
            pltpu.VMEM((1, cols), jnp.float32),
            pltpu.SemaphoreType.DMA((2 * pl.cdiv(rows, min(64, rows)),)),
        ],
        compiler_params=pltpu.CompilerParams(vmem_limit_bytes=20 << 20),
        cost_estimate=pl.CostEstimate(flops=4 * rows * cols, bytes_accessed=16 * rows * cols, transcendentals=0),
        name="finish",
    )(*in_vmem(sums, row_moment[None, :], col_moment, gradient, weight))


def per_device(acts, out_grads, weight, row_state, col_state):
    n_row = lax.axis_size("row")
    n_col = lax.axis_size("col")
    depth = n_row // 4
    width = acts.shape[1]
    tokens = acts.shape[0]
    half, quarter = tokens // 2, tokens // 4
    cols_all = out_grads.shape[1] * n_col
    count_all = width * cols_all
    me = lax.axis_index("row")
    side = lax.axis_index("col") % 2

    def swap(v, bit):
        return lax.ppermute(v, "row", [(i, i ^ bit) for i in range(n_row)])

    def along_z(by, v):
        return lax.ppermute(v, "row", [(i, (i + 4 * by) % n_row) for i in range(n_row)])

    own, pieces = {0: out_grads}, {}
    by_x, by_y = swap(out_grads, 1), swap(out_grads, 2)
    top = swap(by_x[:half], 2)
    pieces[0] = [own[0], by_x, by_y, top, swap(by_y[half:], 1)]
    for k in planes_of(depth):
        by = 1 if 2 * k <= depth else -1
        before = (k - by) % depth
        own[k] = along_z(by, own[before])
        by_x, by_y = swap(own[k], 1), swap(own[k], 2)
        if before == 0:
            far, cut = [along_z(by, top)], half + quarter
            q1, q2 = by_x[half:cut], by_y[cut:]
        else:
            far, q1, q2 = [], by_x[:half], by_y[half:]
        pieces[k] = [own[k], by_x, by_y] + far + [swap(q1, 2), swap(q2, 1)]

    side = side[None]
    blocks = pack(side, acts, n_row)
    blocks = lax.all_to_all(blocks, "row", 0, 0, tiled=True)
    *sooner, last = planes = [0] + planes_of(depth)
    early = [(k, 0) for k in planes] + [(k, j) for k in sooner for j in (1, 2)] + [(0, 3), (last, 1), (last, 2)]
    late = [(k, 3) for k in planes[1:]]
    below = jnp.array([(-k % depth) * 4 for k, _ in early + late], jnp.int32)
    place = jnp.array([j for _, j in early + late], jnp.int32)
    mine = arrange((me - me % 4 + below) % n_row + ((me % 4) ^ place), blocks)
    other = lax.ppermute(mine, "col", [(i, i ^ 1) for i in range(n_col)])
    of = lambda shards: [p for k, j in shards for p in (pieces[k][3:] if j == 3 else [pieces[k][j]])]
    near, far = of(early), of(late)
    gradient, row_squares = last_gemm(side, mine, other, gemm(side, mine, other, near), far)

    row_total = butterfly(row_squares[0], "col", powers(1, n_col))
    row_moment = decay_rate * row_state + (1.0 - decay_rate) * (row_total / cols_all)
    squares = gradient * gradient
    parts = jnp.stack(
        [
            jnp.sum(squares + floor_eps, axis=0),
            jnp.sum(squares * (1.0 / row_moment)[:, None], axis=0),
            jnp.sum(weight * weight, axis=0),
        ]
    )
    totals = parts
    for bit in powers(1, n_row):
        totals = butterfly(totals, "row", [bit])
    col_moment, sums = moments(width, totals, col_state)
    sums = butterfly(sums, "col", powers(1, n_col))
    new_weight, update = finish(count_all, sums, row_moment, col_moment, gradient, weight)
    return (new_weight, update, row_moment, col_moment[0])


def planes_of(depth):
    return [k for i in range(1, depth // 2) for k in (i, depth - i)] + [depth // 2]


def solution(mesh):
    return jax.shard_map(
        per_device,
        mesh=mesh,
        in_specs=(P("row", None), P("row", "col"), P("row", "col"), P("row"), P("col")),
        out_specs=(P("row", "col"), P("row", "col"), P("row"), P("col")),
        check_vma=False,
    )
```

```python
import functools

import jax
import jax.numpy as jnp
from jax import lax
from jax.experimental import pallas as pl
from jax.experimental.pallas import tpu as pltpu
from jax.sharding import PartitionSpec as P

decay_rate = 0.85
floor_eps = 1e-30
relative_rate = 0.05
LANES = 128


def spans(offsets):
    out = [0]
    for offset in offsets:
        out = out + [offset ^ s for s in out]
    return out


def butterfly(value, axis, offsets):
    n = lax.axis_size(axis)
    terms = [value] + [lax.ppermute(value, axis, [(i, i ^ s) for i in range(n)]) for s in spans(offsets)[1:]]
    while len(terms) > 1:
        terms = [a + b for a, b in zip(terms[::2], terms[1::2])]
    return terms[0]


def powers(first, end):
    out = []
    while first < end:
        out.append(first)
        first *= 2
    return out


def placed(space, arrays):
    return [pltpu.with_memory_space_constraint(a, space) for a in arrays]


def in_vmem(*arrays):
    return placed(pltpu.VMEM, arrays)


WHOLE = pl.BlockSpec(memory_space=pltpu.VMEM)
SCALARS = pl.BlockSpec(memory_space=pltpu.SMEM)


def pack_kernel(side_ref, acts_ref, out_ref):
    _, _, width = out_ref.shape
    low = side_ref[0] == 0
    for d in range(out_ref.shape[0]):
        at = 2 * d * width
        a, b = acts_ref[:, at : at + width], acts_ref[:, at + width : at + 2 * width]
        out_ref[d] = jnp.where(low, a, b)


def pack(side, acts, n_row):
    tokens, width = acts.shape
    return pl.pallas_call(
        pack_kernel,
        out_shape=jax.ShapeDtypeStruct((n_row, tokens, width // (2 * n_row)), acts.dtype),
        in_specs=[SCALARS, WHOLE],
        out_specs=WHOLE,
        compiler_params=pltpu.CompilerParams(vmem_limit_bytes=12 << 20),
        cost_estimate=pl.CostEstimate(flops=0, bytes_accessed=3 * acts.size, transcendentals=0),
        name="pack",
    )(side, acts)


def arrange_kernel(index_ref, blocks_ref, out_ref):
    n_row, tokens, _ = blocks_ref.shape
    for s in range(n_row):
        out_ref[:, s * tokens : (s + 1) * tokens] = blocks_ref[index_ref[s]].T


def arrange(index, blocks):
    n_row, tokens, rows = blocks.shape
    return pl.pallas_call(
        arrange_kernel,
        out_shape=pltpu.VMEM((rows, n_row * tokens), blocks.dtype),
        in_specs=[SCALARS, WHOLE],
        out_specs=WHOLE,
        compiler_params=pltpu.CompilerParams(vmem_limit_bytes=12 << 20),
        cost_estimate=pl.CostEstimate(flops=0, bytes_accessed=8 * blocks.size, transcendentals=0),
        name="arrange",
    )(index, *in_vmem(blocks))


def fill(slab, pieces, lanes):
    at = 0
    for piece in pieces:
        slab[at : at + piece.shape[0], :] = piece[:, lanes]
        at += piece.shape[0]


def gemm_kernel(side_ref, mine_ref, other_ref, *refs):
    *pieces, out_ref, slab = refs
    depth = slab.shape[0]
    height = mine_ref.shape[0]
    fill(slab, pieces, slice(None))
    for at, columns_ref in ((side_ref[0], mine_ref), (1 - side_ref[0], other_ref)):
        rows = pl.ds(pl.multiple_of(at * height, height), height)
        out_ref[rows, :] = jnp.dot(columns_ref[:, :depth], slab[...], preferred_element_type=jnp.float32)


def gemm(side, mine, other, pieces):
    rows = 2 * mine.shape[0]
    depth = sum(p.shape[0] for p in pieces)
    cols = pieces[0].shape[1]
    width = min(512, cols)
    return pl.pallas_call(
        gemm_kernel,
        grid=(cols // width,),
        out_shape=jax.ShapeDtypeStruct((rows, cols), jnp.float32),
        in_specs=[SCALARS, WHOLE, WHOLE] + [pl.BlockSpec((p.shape[0], width), lambda j: (0, j)) for p in pieces],
        out_specs=pl.BlockSpec((rows, width), lambda j: (0, j)),
        scratch_shapes=[pltpu.VMEM((depth, width), jnp.bfloat16)],
        compiler_params=pltpu.CompilerParams(vmem_limit_bytes=24 << 20),
        cost_estimate=pl.CostEstimate(flops=2 * rows * depth * cols, bytes_accessed=2 * depth * cols, transcendentals=0),
        name="gemm",
    )(side, *in_vmem(mine, other), *placed(pltpu.HBM, pieces))


def last_kernel(side_ref, mine_ref, other_ref, before_ref, *refs):
    *pieces, out_ref, rows_ref, slab, sums = refs
    depth, width = slab.shape
    height = mine_ref.shape[0]
    first = mine_ref.shape[1] - depth
    cols = out_ref.shape[1]
    side = side_ref[0]
    for t in range(0, cols, width):
        lanes = slice(t, t + width)
        fill(slab, pieces, lanes)
        for at, columns_ref in ((side, mine_ref), (1 - side, other_ref)):
            rows = pl.ds(pl.multiple_of(at * height, height), height)
            total = before_ref[rows, lanes] + jnp.dot(
                columns_ref[:, first:], slab[...], preferred_element_type=jnp.float32
            )
            out_ref[rows, lanes] = total
            squares = total * total + floor_eps
            part = squares[:, :LANES]
            for u in range(LANES, width, LANES):
                part = part + squares[:, u : u + LANES]
            sums[rows, :] = part if t == 0 else sums[rows, :] + part
    rows_ref[...] = jnp.sum(sums[...].T, axis=0, keepdims=True)


def last_gemm(side, mine, other, before, pieces):
    rows, cols = before.shape
    depth = sum(p.shape[0] for p in pieces)
    return pl.pallas_call(
        last_kernel,
        out_shape=[pltpu.VMEM((rows, cols), jnp.float32), pltpu.VMEM((1, rows), jnp.float32)],
        in_specs=[SCALARS] + [WHOLE] * (3 + len(pieces)),
        out_specs=[WHOLE, WHOLE],
        scratch_shapes=[pltpu.VMEM((depth, min(512, cols)), jnp.bfloat16), pltpu.VMEM((rows, LANES), jnp.float32)],
        compiler_params=pltpu.CompilerParams(vmem_limit_bytes=24 << 20),
        cost_estimate=pl.CostEstimate(flops=2 * rows * depth * cols, bytes_accessed=2 * depth * cols, transcendentals=0),
        name="last_gemm",
    )(side, *in_vmem(mine, other, before, *pieces[:2]), *pieces[2:])


def moments_kernel(height, totals_ref, state_ref, col_ref, sums_ref):
    cols = state_ref.shape[1]
    col = decay_rate * state_ref[...] + (1.0 - decay_rate) * (totals_ref[0:1, :cols] / height)
    col_ref[...] = col
    clip = jnp.sum(totals_ref[1:2, :cols] / col)
    weight = jnp.sum(totals_ref[0:1, cols:])
    row = lax.broadcasted_iota(jnp.int32, sums_ref.shape, 0)
    sums_ref[...] = jnp.where(row == 0, clip, weight)


def moments(height, totals, col_state):
    cols = col_state.shape[0]
    whole = pl.BlockSpec(memory_space=pltpu.VMEM)
    return pl.pallas_call(
        functools.partial(moments_kernel, height),
        out_shape=[pltpu.VMEM((1, cols), jnp.float32), pltpu.VMEM((8, LANES), jnp.float32)],
        in_specs=[whole, whole],
        out_specs=[whole, whole],
        compiler_params=pltpu.CompilerParams(vmem_limit_bytes=8 << 20),
        name="moments",
    )(totals, col_state[None, :])


def finish_kernel(count_all, sums_ref, row_ref, col_ref, gradient_ref, weight_ref, new_hbm, update_hbm, new, update, rows, cols, sems):
    clip = jnp.maximum(1.0, jnp.sqrt(sums_ref[0:1, :] / count_all))
    step_size = relative_rate * jnp.sqrt(sums_ref[1:2, :] / count_all + 1e-06)
    root = lax.rsqrt(row_ref[...])
    rows[...] = jnp.broadcast_to(root, (LANES, root.shape[1])).T
    for t in range(0, cols.shape[1], LANES):
        cols[:, t : t + LANES] = lax.rsqrt(col_ref[:, t : t + LANES]) / clip
    height = min(64, rows.shape[0])
    copies = []
    for i in range(rows.shape[0] // height):
        here = slice(i * height, (i + 1) * height)
        scale = rows[here, :]
        for t in range(0, cols.shape[1], LANES):
            lanes = slice(t, t + LANES)
            value = gradient_ref[here, lanes] * scale * cols[:, lanes]
            update[here, lanes] = value
            new[here, lanes] = weight_ref[here, lanes] - step_size * value
        for j, (source, target) in enumerate(((update, update_hbm), (new, new_hbm))):
            copies.append(pltpu.make_async_copy(source.at[here], target.at[here], sems.at[2 * i + j]))
            copies[-1].start()
    for copy in copies:
        copy.wait()


def finish(count_all, sums, row_moment, col_moment, gradient, weight):
    rows, cols = gradient.shape
    out = pltpu.HBM((rows, cols), jnp.float32)
    there = pl.BlockSpec(memory_space=pl.ANY)
    return pl.pallas_call(
        functools.partial(finish_kernel, count_all),
        out_shape=[out, out],
        in_specs=[WHOLE] * 5,
        out_specs=[there, there],
        scratch_shapes=[
            pltpu.VMEM((rows, cols), jnp.float32),
            pltpu.VMEM((rows, cols), jnp.float32),
            pltpu.VMEM((rows, LANES), jnp.float32),
            pltpu.VMEM((1, cols), jnp.float32),
            pltpu.SemaphoreType.DMA((2 * pl.cdiv(rows, min(64, rows)),)),
        ],
        compiler_params=pltpu.CompilerParams(vmem_limit_bytes=20 << 20),
        cost_estimate=pl.CostEstimate(flops=4 * rows * cols, bytes_accessed=16 * rows * cols, transcendentals=0),
        name="finish",
    )(*in_vmem(sums, row_moment[None, :], col_moment, gradient, weight))


def per_device(acts, out_grads, weight, row_state, col_state):
    n_row = lax.axis_size("row")
    n_col = lax.axis_size("col")
    depth = n_row // 4
    width = acts.shape[1]
    tokens = acts.shape[0]
    half, quarter = tokens // 2, tokens // 4
    cols_all = out_grads.shape[1] * n_col
    count_all = width * cols_all
    me = lax.axis_index("row")
    side = lax.axis_index("col") % 2

    def swap(v, bit):
        return lax.ppermute(v, "row", [(i, i ^ bit) for i in range(n_row)])

    def along_z(by, v):
        return lax.ppermute(v, "row", [(i, (i + 4 * by) % n_row) for i in range(n_row)])

    own, pieces = {0: out_grads}, {}
    by_x, by_y = swap(out_grads, 1), swap(out_grads, 2)
    top = swap(by_x[:half], 2)
    pieces[0] = [own[0], by_x, by_y, top, swap(by_y[half:], 1)]
    for k in planes_of(depth):
        by = 1 if 2 * k <= depth else -1
        before = (k - by) % depth
        own[k] = along_z(by, own[before])
        by_x, by_y = swap(own[k], 1), swap(own[k], 2)
        if before == 0:
            far, cut = [along_z(by, top)], half + quarter
            q1, q2 = by_x[half:cut], by_y[cut:]
        else:
            far, q1, q2 = [], by_x[:half], by_y[half:]
        pieces[k] = [own[k], by_x, by_y] + far + [swap(q1, 2), swap(q2, 1)]

    side = side[None]
    blocks = pack(side, acts, n_row)
    blocks = lax.all_to_all(blocks, "row", 0, 0, tiled=True)
    *sooner, last = planes = [0] + planes_of(depth)
    early = [(k, 0) for k in planes] + [(k, j) for k in sooner for j in (1, 2)] + [(0, 3)]
    late = [(last, 1), (last, 2)] + [(k, 3) for k in planes[1:]]
    below = jnp.array([(-k % depth) * 4 for k, _ in early + late], jnp.int32)
    place = jnp.array([j for _, j in early + late], jnp.int32)
    mine = arrange((me - me % 4 + below) % n_row + ((me % 4) ^ place), blocks)
    other = lax.ppermute(mine, "col", [(i, i ^ 1) for i in range(n_col)])
    of = lambda shards: [p for k, j in shards for p in (pieces[k][3:] if j == 3 else [pieces[k][j]])]
    near, far = of(early), of(late)
    gradient, row_squares = last_gemm(side, mine, other, gemm(side, mine, other, near), far)

    row_total = butterfly(row_squares[0], "col", powers(1, n_col))
    row_moment = decay_rate * row_state + (1.0 - decay_rate) * (row_total / cols_all)
    squares = gradient * gradient
    spare = jnp.sum(weight * weight, axis=0)
    spare = jnp.sum(spare.reshape(-1, LANES), axis=0)
    totals = jnp.stack(
        [
            jnp.concatenate([jnp.sum(squares + floor_eps, axis=0), spare]),
            jnp.concatenate([jnp.sum(squares * (1.0 / row_moment)[:, None], axis=0), jnp.zeros_like(spare)]),
        ]
    )
    totals = butterfly(totals, "row", [1, 2])
    for bit in powers(4, n_row):
        totals = butterfly(totals, "row", [bit])
    col_moment, sums = moments(width, totals, col_state)
    sums = butterfly(sums, "col", powers(1, n_col))
    new_weight, update = finish(count_all, sums, row_moment, col_moment, gradient, weight)
    return (new_weight, update, row_moment, col_moment[0])


def planes_of(depth):
    return [k for i in range(1, depth // 2) for k in (i, depth - i)] + [depth // 2]


def solution(mesh):
    return jax.shard_map(
        per_device,
        mesh=mesh,
        in_specs=(P("row", None), P("row", "col"), P("row", "col"), P("row"), P("col")),
        out_specs=(P("row", "col"), P("row", "col"), P("row"), P("col")),
        check_vma=False,
    )
```

```python
import functools

import jax
import jax.numpy as jnp
from jax import lax
from jax.experimental import pallas as pl
from jax.experimental.pallas import tpu as pltpu
from jax.sharding import PartitionSpec as P

decay_rate = 0.85
floor_eps = 1e-30
relative_rate = 0.05
LANES = 128


def spans(offsets):
    out = [0]
    for offset in offsets:
        out = out + [offset ^ s for s in out]
    return out


def butterfly(value, axis, offsets):
    n = lax.axis_size(axis)
    terms = [value]
    for s in spans(offsets)[1:]:
        terms.append(lax.ppermute(value, axis, [(i, i ^ s) for i in range(n)]))
    while len(terms) > 1:
        terms = [a + b for a, b in zip(terms[::2], terms[1::2])]
    return terms[0]


def powers(first, end):
    out = []
    while first < end:
        out.append(first)
        first *= 2
    return out


def placed(space, arrays):
    return [pltpu.with_memory_space_constraint(a, space) for a in arrays]


def in_vmem(*arrays):
    return placed(pltpu.VMEM, arrays)


WHOLE = pl.BlockSpec(memory_space=pltpu.VMEM)
SCALARS = pl.BlockSpec(memory_space=pltpu.SMEM)


def pack_kernel(side_ref, acts_ref, out_ref):
    _, _, width = out_ref.shape
    low = side_ref[0] == 0
    for d in range(out_ref.shape[0]):
        at = 2 * d * width
        a, b = acts_ref[:, at : at + width], acts_ref[:, at + width : at + 2 * width]
        out_ref[d] = jnp.where(low, a, b)


def pack(side, acts, n_row):
    tokens, width = acts.shape
    return pl.pallas_call(
        pack_kernel,
        out_shape=jax.ShapeDtypeStruct((n_row, tokens, width // (2 * n_row)), acts.dtype),
        in_specs=[SCALARS, WHOLE],
        out_specs=WHOLE,
        compiler_params=pltpu.CompilerParams(vmem_limit_bytes=12 << 20),
        cost_estimate=pl.CostEstimate(flops=0, bytes_accessed=3 * acts.size, transcendentals=0),
        name="pack",
    )(side, acts)


def arrange_kernel(index_ref, blocks_ref, out_ref):
    n_row, tokens, _ = blocks_ref.shape
    for s in range(n_row):
        out_ref[:, s * tokens : (s + 1) * tokens] = blocks_ref[index_ref[s]].T


def arrange(index, blocks):
    n_row, tokens, rows = blocks.shape
    return pl.pallas_call(
        arrange_kernel,
        out_shape=pltpu.VMEM((rows, n_row * tokens), blocks.dtype),
        in_specs=[SCALARS, WHOLE],
        out_specs=WHOLE,
        compiler_params=pltpu.CompilerParams(vmem_limit_bytes=12 << 20),
        cost_estimate=pl.CostEstimate(flops=0, bytes_accessed=8 * blocks.size, transcendentals=0),
        name="arrange",
    )(index, *in_vmem(blocks))


def fill(slab, pieces, lanes):
    at = 0
    for piece in pieces:
        slab[at : at + piece.shape[0], :] = piece[:, lanes]
        at += piece.shape[0]


def gemm_kernel(side_ref, mine_ref, other_ref, *refs):
    *pieces, out_ref, slab = refs
    depth = slab.shape[0]
    height = mine_ref.shape[0]
    fill(slab, pieces, slice(None))
    for at, columns_ref in ((side_ref[0], mine_ref), (1 - side_ref[0], other_ref)):
        rows = pl.ds(pl.multiple_of(at * height, height), height)
        out_ref[rows, :] = jnp.dot(columns_ref[:, :depth], slab[...], preferred_element_type=jnp.float32)


def gemm(side, mine, other, pieces):
    rows = 2 * mine.shape[0]
    depth = sum(p.shape[0] for p in pieces)
    cols = pieces[0].shape[1]
    width = min(512, cols)
    return pl.pallas_call(
        gemm_kernel,
        grid=(cols // width,),
        out_shape=jax.ShapeDtypeStruct((rows, cols), jnp.float32),
        in_specs=[SCALARS, WHOLE, WHOLE] + [pl.BlockSpec((p.shape[0], width), lambda j: (0, j)) for p in pieces],
        out_specs=pl.BlockSpec((rows, width), lambda j: (0, j)),
        scratch_shapes=[pltpu.VMEM((depth, width), jnp.bfloat16)],
        compiler_params=pltpu.CompilerParams(vmem_limit_bytes=24 << 20),
        cost_estimate=pl.CostEstimate(flops=2 * rows * depth * cols, bytes_accessed=2 * depth * cols, transcendentals=0),
        name="gemm",
    )(side, *in_vmem(mine, other), *placed(pltpu.HBM, pieces))


def last_kernel(side_ref, mine_ref, other_ref, before_ref, *refs):
    *pieces, out_ref, rows_ref, slab, sums = refs
    depth, width = slab.shape
    height = mine_ref.shape[0]
    first = mine_ref.shape[1] - depth
    cols = out_ref.shape[1]
    side = side_ref[0]
    for t in range(0, cols, width):
        lanes = slice(t, t + width)
        fill(slab, pieces, lanes)
        for at, columns_ref in ((side, mine_ref), (1 - side, other_ref)):
            rows = pl.ds(pl.multiple_of(at * height, height), height)
            total = before_ref[rows, lanes] + jnp.dot(
                columns_ref[:, first:], slab[...], preferred_element_type=jnp.float32
            )
            out_ref[rows, lanes] = total
            squares = total * total + floor_eps
            part = squares[:, :LANES]
            for u in range(LANES, width, LANES):
                part = part + squares[:, u : u + LANES]
            sums[rows, :] = part if t == 0 else sums[rows, :] + part
    rows_ref[...] = jnp.sum(sums[...].T, axis=0, keepdims=True)


def last_gemm(side, mine, other, before, pieces):
    rows, cols = before.shape
    depth = sum(p.shape[0] for p in pieces)
    return pl.pallas_call(
        last_kernel,
        out_shape=[pltpu.VMEM((rows, cols), jnp.float32), pltpu.VMEM((1, rows), jnp.float32)],
        in_specs=[SCALARS] + [WHOLE] * (3 + len(pieces)),
        out_specs=[WHOLE, WHOLE],
        scratch_shapes=[pltpu.VMEM((depth, min(512, cols)), jnp.bfloat16), pltpu.VMEM((rows, LANES), jnp.float32)],
        compiler_params=pltpu.CompilerParams(vmem_limit_bytes=24 << 20),
        cost_estimate=pl.CostEstimate(flops=2 * rows * depth * cols, bytes_accessed=2 * depth * cols, transcendentals=0),
        name="last_gemm",
    )(side, *in_vmem(mine, other, before, *pieces[:2]), *pieces[2:])


def moments_kernel(height, totals_ref, state_ref, col_ref, sums_ref):
    cols = state_ref.shape[1]
    col = decay_rate * state_ref[...] + (1.0 - decay_rate) * (totals_ref[0:1, :cols] / height)
    col_ref[...] = col
    clip = jnp.sum(totals_ref[1:2, :cols] / col)
    weight = jnp.sum(totals_ref[0:1, cols:])
    row = lax.broadcasted_iota(jnp.int32, sums_ref.shape, 0)
    sums_ref[...] = jnp.where(row == 0, clip, weight)


def moments(height, totals, col_state):
    cols = col_state.shape[0]
    whole = pl.BlockSpec(memory_space=pltpu.VMEM)
    return pl.pallas_call(
        functools.partial(moments_kernel, height),
        out_shape=[pltpu.VMEM((1, cols), jnp.float32), pltpu.VMEM((8, LANES), jnp.float32)],
        in_specs=[whole, whole],
        out_specs=[whole, whole],
        compiler_params=pltpu.CompilerParams(vmem_limit_bytes=8 << 20),
        name="moments",
    )(totals, col_state[None, :])


def finish_kernel(count_all, sums_ref, row_ref, col_ref, gradient_ref, weight_ref, new_hbm, update_hbm, new, update, rows, cols, sems):
    clip = jnp.maximum(1.0, jnp.sqrt(sums_ref[0:1, :] / count_all))
    step_size = relative_rate * jnp.sqrt(sums_ref[1:2, :] / count_all + 1e-06)
    root = lax.rsqrt(row_ref[...])
    rows[...] = jnp.broadcast_to(root, (LANES, root.shape[1])).T
    for t in range(0, cols.shape[1], LANES):
        cols[:, t : t + LANES] = lax.rsqrt(col_ref[:, t : t + LANES]) / clip
    height = min(64, rows.shape[0])
    copies = []
    for i in range(rows.shape[0] // height):
        here = slice(i * height, (i + 1) * height)
        scale = rows[here, :]
        for t in range(0, cols.shape[1], LANES):
            lanes = slice(t, t + LANES)
            value = gradient_ref[here, lanes] * scale * cols[:, lanes]
            update[here, lanes] = value
            new[here, lanes] = weight_ref[here, lanes] - step_size * value
        for j, (source, target) in enumerate(((update, update_hbm), (new, new_hbm))):
            copies.append(pltpu.make_async_copy(source.at[here], target.at[here], sems.at[2 * i + j]))
            copies[-1].start()
    for copy in copies:
        copy.wait()


def finish(count_all, sums, row_moment, col_moment, gradient, weight):
    rows, cols = gradient.shape
    out = pltpu.HBM((rows, cols), jnp.float32)
    there = pl.BlockSpec(memory_space=pl.ANY)
    return pl.pallas_call(
        functools.partial(finish_kernel, count_all),
        out_shape=[out, out],
        in_specs=[WHOLE] * 5,
        out_specs=[there, there],
        scratch_shapes=[
            pltpu.VMEM((rows, cols), jnp.float32),
            pltpu.VMEM((rows, cols), jnp.float32),
            pltpu.VMEM((rows, LANES), jnp.float32),
            pltpu.VMEM((1, cols), jnp.float32),
            pltpu.SemaphoreType.DMA((2 * pl.cdiv(rows, min(64, rows)),)),
        ],
        compiler_params=pltpu.CompilerParams(vmem_limit_bytes=20 << 20),
        cost_estimate=pl.CostEstimate(flops=4 * rows * cols, bytes_accessed=16 * rows * cols, transcendentals=0),
        name="finish",
    )(*in_vmem(sums, row_moment[None, :], col_moment, gradient, weight))


def per_device(acts, out_grads, weight, row_state, col_state):
    n_row = lax.axis_size("row")
    n_col = lax.axis_size("col")
    depth = n_row // 4
    width = acts.shape[1]
    tokens = acts.shape[0]
    half, quarter = tokens // 2, tokens // 4
    cols_all = out_grads.shape[1] * n_col
    count_all = width * cols_all
    me = lax.axis_index("row")
    side = lax.axis_index("col") % 2

    def swap(v, bit):
        return lax.ppermute(v, "row", [(i, i ^ bit) for i in range(n_row)])

    def along_z(by, v):
        return lax.ppermute(v, "row", [(i, (i + 4 * by) % n_row) for i in range(n_row)])

    own, pieces = {0: out_grads}, {}
    by_x, by_y = swap(out_grads, 1), swap(out_grads, 2)
    top = swap(by_x[:half], 2)
    pieces[0] = [own[0], by_x, by_y, top, swap(by_y[half:], 1)]
    for k in planes_of(depth):
        by = 1 if 2 * k <= depth else -1
        before = (k - by) % depth
        own[k] = along_z(by, own[before])
        by_x, by_y = swap(own[k], 1), swap(own[k], 2)
        if before == 0:
            far, cut = [along_z(by, top)], half + quarter
            q1, q2 = by_x[half:cut], by_y[cut:]
        else:
            far, q1, q2 = [], by_x[:half], by_y[half:]
        pieces[k] = [own[k], by_x, by_y] + far + [swap(q1, 2), swap(q2, 1)]

    side = side[None]
    blocks = pack(side, acts, n_row)
    blocks = lax.all_to_all(blocks, "row", 0, 0, tiled=True)
    *sooner, last = planes = [0] + planes_of(depth)
    early = [(k, 0) for k in planes] + [(k, j) for k in sooner for j in (1, 2)] + [(0, 3)]
    late = [(last, 1), (last, 2)] + [(k, 3) for k in planes[1:]]
    below = jnp.array([(-k % depth) * 4 for k, _ in early + late], jnp.int32)
    place = jnp.array([j for _, j in early + late], jnp.int32)
    mine = arrange((me - me % 4 + below) % n_row + ((me % 4) ^ place), blocks)
    other = lax.ppermute(mine, "col", [(i, i ^ 1) for i in range(n_col)])
    of = lambda shards: [p for k, j in shards for p in (pieces[k][3:] if j == 3 else [pieces[k][j]])]
    near, far = of(early), of(late)
    gradient, row_squares = last_gemm(side, mine, other, gemm(side, mine, other, near), far)

    row_total = butterfly(row_squares[0], "col", powers(1, n_col))
    row_moment = decay_rate * row_state + (1.0 - decay_rate) * (row_total / cols_all)
    squares = gradient * gradient
    spare = jnp.sum(weight * weight, axis=0)
    spare = jnp.sum(spare.reshape(-1, LANES), axis=0)
    totals = jnp.stack(
        [
            jnp.concatenate([jnp.sum(squares + floor_eps, axis=0), spare]),
            jnp.concatenate([jnp.sum(squares * (1.0 / row_moment)[:, None], axis=0), jnp.zeros_like(spare)]),
        ]
    )
    totals = butterfly(butterfly(totals, "row", [1, 2]), "row", powers(4, n_row))
    col_moment, sums = moments(width, totals, col_state)
    sums = butterfly(sums, "col", powers(1, n_col))
    new_weight, update = finish(count_all, sums, row_moment, col_moment, gradient, weight)
    return (new_weight, update, row_moment, col_moment[0])


def planes_of(depth):
    return [k for i in range(1, depth // 2) for k in (i, depth - i)] + [depth // 2]


def solution(mesh):
    return jax.shard_map(
        per_device,
        mesh=mesh,
        in_specs=(P("row", None), P("row", "col"), P("row", "col"), P("row"), P("col")),
        out_specs=(P("row", "col"), P("row", "col"), P("row"), P("col")),
        check_vma=False,
    )
```

```python
import functools

import jax
import jax.numpy as jnp
from jax import lax
from jax.experimental import pallas as pl
from jax.experimental.pallas import tpu as pltpu
from jax.sharding import PartitionSpec as P

decay_rate = 0.85
floor_eps = 1e-30
relative_rate = 0.05
LANES = 128


def spans(offsets):
    out = [0]
    for offset in offsets:
        out = out + [offset ^ s for s in out]
    return out


def butterfly(value, axis, offsets):
    n = lax.axis_size(axis)
    terms = [value]
    for s in spans(offsets)[1:]:
        terms.append(lax.ppermute(value, axis, [(i, i ^ s) for i in range(n)]))
    while len(terms) > 1:
        terms = [a + b for a, b in zip(terms[::2], terms[1::2])]
    return terms[0]


def powers(first, end):
    out = []
    while first < end:
        out.append(first)
        first *= 2
    return out


def placed(space, arrays):
    return [pltpu.with_memory_space_constraint(a, space) for a in arrays]


def in_vmem(*arrays):
    return placed(pltpu.VMEM, arrays)


WHOLE = pl.BlockSpec(memory_space=pltpu.VMEM)
SCALARS = pl.BlockSpec(memory_space=pltpu.SMEM)


def pack_kernel(side_ref, acts_ref, out_ref):
    _, _, width = out_ref.shape
    low = side_ref[0] == 0
    for d in range(out_ref.shape[0]):
        at = 2 * d * width
        a, b = acts_ref[:, at : at + width], acts_ref[:, at + width : at + 2 * width]
        out_ref[d] = jnp.where(low, a, b)


def pack(side, acts, n_row):
    tokens, width = acts.shape
    return pl.pallas_call(
        pack_kernel,
        out_shape=jax.ShapeDtypeStruct((n_row, tokens, width // (2 * n_row)), acts.dtype),
        in_specs=[SCALARS, WHOLE],
        out_specs=WHOLE,
        compiler_params=pltpu.CompilerParams(vmem_limit_bytes=12 << 20),
        cost_estimate=pl.CostEstimate(flops=0, bytes_accessed=3 * acts.size, transcendentals=0),
        name="pack",
    )(side, acts)


def arrange_kernel(index_ref, blocks_ref, out_ref):
    n_row, tokens, _ = blocks_ref.shape
    for s in range(n_row):
        out_ref[:, s * tokens : (s + 1) * tokens] = blocks_ref[index_ref[s]].T


def arrange(index, blocks):
    n_row, tokens, rows = blocks.shape
    return pl.pallas_call(
        arrange_kernel,
        out_shape=pltpu.VMEM((rows, n_row * tokens), blocks.dtype),
        in_specs=[SCALARS, WHOLE],
        out_specs=WHOLE,
        compiler_params=pltpu.CompilerParams(vmem_limit_bytes=12 << 20),
        cost_estimate=pl.CostEstimate(flops=0, bytes_accessed=8 * blocks.size, transcendentals=0),
        name="arrange",
    )(index, *in_vmem(blocks))


def fill(slab, pieces, lanes):
    at = 0
    for piece in pieces:
        slab[at : at + piece.shape[0], :] = piece[:, lanes]
        at += piece.shape[0]


def gemm_kernel(side_ref, mine_ref, other_ref, *refs):
    *pieces, out_ref, slab, sems = refs
    depth, cols = slab.shape
    height = mine_ref.shape[0]
    width = min(512, cols)
    blocks = [slice(t, t + width) for t in range(0, cols, width)]
    copies = []
    for t, lanes in enumerate(blocks):
        at = 0
        for p, piece in enumerate(pieces):
            here = slice(at, at + piece.shape[0])
            sem = sems.at[t * len(pieces) + p]
            copies.append(pltpu.make_async_copy(piece.at[:, lanes], slab.at[here, lanes], sem))
            copies[-1].start()
            at += piece.shape[0]
    for t, lanes in enumerate(blocks):
        for copy in copies[t * len(pieces) : (t + 1) * len(pieces)]:
            copy.wait()
        for at, columns_ref in ((side_ref[0], mine_ref), (1 - side_ref[0], other_ref)):
            rows = pl.ds(pl.multiple_of(at * height, height), height)
            out_ref[rows, lanes] = jnp.dot(columns_ref[:, :depth], slab[:, lanes], preferred_element_type=jnp.float32)


def gemm(side, mine, other, pieces):
    rows = 2 * mine.shape[0]
    depth = sum(p.shape[0] for p in pieces)
    cols = pieces[0].shape[1]
    return pl.pallas_call(
        gemm_kernel,
        out_shape=pltpu.VMEM((rows, cols), jnp.float32),
        in_specs=[SCALARS, WHOLE, WHOLE] + [pl.BlockSpec(memory_space=pl.ANY)] * (len(pieces) - 2) + [WHOLE] * 2,
        out_specs=WHOLE,
        scratch_shapes=[
            pltpu.VMEM((depth, cols), jnp.bfloat16),
            pltpu.SemaphoreType.DMA((len(pieces) * pl.cdiv(cols, 512),)),
        ],
        compiler_params=pltpu.CompilerParams(vmem_limit_bytes=24 << 20),
        cost_estimate=pl.CostEstimate(flops=2 * rows * depth * cols, bytes_accessed=2 * depth * cols, transcendentals=0),
        name="gemm",
    )(side, *in_vmem(mine, other), *placed(pltpu.HBM, pieces[:-2]), *in_vmem(*pieces[-2:]))


def last_kernel(side_ref, mine_ref, other_ref, before_ref, *refs):
    *pieces, out_ref, rows_ref, slab, sums = refs
    depth, width = slab.shape
    height = mine_ref.shape[0]
    first = mine_ref.shape[1] - depth
    cols = out_ref.shape[1]
    side = side_ref[0]
    for t in range(0, cols, width):
        lanes = slice(t, t + width)
        fill(slab, pieces, lanes)
        for at, columns_ref in ((side, mine_ref), (1 - side, other_ref)):
            rows = pl.ds(pl.multiple_of(at * height, height), height)
            total = before_ref[rows, lanes] + jnp.dot(
                columns_ref[:, first:], slab[...], preferred_element_type=jnp.float32
            )
            out_ref[rows, lanes] = total
            squares = total * total + floor_eps
            part = squares[:, :LANES]
            for u in range(LANES, width, LANES):
                part = part + squares[:, u : u + LANES]
            sums[rows, :] = part if t == 0 else sums[rows, :] + part
    rows_ref[...] = jnp.sum(sums[...].T, axis=0, keepdims=True)


def last_gemm(side, mine, other, before, pieces):
    rows, cols = before.shape
    depth = sum(p.shape[0] for p in pieces)
    return pl.pallas_call(
        last_kernel,
        out_shape=[pltpu.VMEM((rows, cols), jnp.float32), pltpu.VMEM((1, rows), jnp.float32)],
        in_specs=[SCALARS] + [WHOLE] * (3 + len(pieces)),
        out_specs=[WHOLE, WHOLE],
        scratch_shapes=[pltpu.VMEM((depth, min(512, cols)), jnp.bfloat16), pltpu.VMEM((rows, LANES), jnp.float32)],
        compiler_params=pltpu.CompilerParams(vmem_limit_bytes=24 << 20),
        cost_estimate=pl.CostEstimate(flops=2 * rows * depth * cols, bytes_accessed=2 * depth * cols, transcendentals=0),
        name="last_gemm",
    )(side, *in_vmem(mine, other, before), *pieces)


def moments_kernel(height, totals_ref, state_ref, col_ref, sums_ref):
    cols = state_ref.shape[1]
    col = decay_rate * state_ref[...] + (1.0 - decay_rate) * (totals_ref[0:1, :cols] / height)
    col_ref[...] = col
    clip = jnp.sum(totals_ref[1:2, :cols] / col)
    weight = jnp.sum(totals_ref[0:1, cols:])
    row = lax.broadcasted_iota(jnp.int32, sums_ref.shape, 0)
    sums_ref[...] = jnp.where(row == 0, clip, weight)


def moments(height, totals, col_state):
    cols = col_state.shape[0]
    whole = pl.BlockSpec(memory_space=pltpu.VMEM)
    return pl.pallas_call(
        functools.partial(moments_kernel, height),
        out_shape=[pltpu.VMEM((1, cols), jnp.float32), pltpu.VMEM((8, LANES), jnp.float32)],
        in_specs=[whole, whole],
        out_specs=[whole, whole],
        compiler_params=pltpu.CompilerParams(vmem_limit_bytes=8 << 20),
        name="moments",
    )(totals, col_state[None, :])


def finish_kernel(count_all, sums_ref, row_ref, col_ref, gradient_ref, weight_ref, new_hbm, update_hbm, new, update, rows, cols, sems):
    clip = jnp.maximum(1.0, jnp.sqrt(sums_ref[0:1, :] / count_all))
    step_size = relative_rate * jnp.sqrt(sums_ref[1:2, :] / count_all + 1e-06)
    root = lax.rsqrt(row_ref[...])
    rows[...] = jnp.broadcast_to(root, (LANES, root.shape[1])).T
    for t in range(0, cols.shape[1], LANES):
        cols[:, t : t + LANES] = lax.rsqrt(col_ref[:, t : t + LANES]) / clip
    height = min(64, rows.shape[0])
    copies = []
    for i in range(rows.shape[0] // height):
        here = slice(i * height, (i + 1) * height)
        scale = rows[here, :]
        for t in range(0, cols.shape[1], LANES):
            lanes = slice(t, t + LANES)
            value = gradient_ref[here, lanes] * scale * cols[:, lanes]
            update[here, lanes] = value
            new[here, lanes] = weight_ref[here, lanes] - step_size * value
        for j, (source, target) in enumerate(((update, update_hbm), (new, new_hbm))):
            copies.append(pltpu.make_async_copy(source.at[here], target.at[here], sems.at[2 * i + j]))
            copies[-1].start()
    for copy in copies:
        copy.wait()


def finish(count_all, sums, row_moment, col_moment, gradient, weight):
    rows, cols = gradient.shape
    out = pltpu.HBM((rows, cols), jnp.float32)
    there = pl.BlockSpec(memory_space=pl.ANY)
    return pl.pallas_call(
        functools.partial(finish_kernel, count_all),
        out_shape=[out, out],
        in_specs=[WHOLE] * 5,
        out_specs=[there, there],
        scratch_shapes=[
            pltpu.VMEM((rows, cols), jnp.float32),
            pltpu.VMEM((rows, cols), jnp.float32),
            pltpu.VMEM((rows, LANES), jnp.float32),
            pltpu.VMEM((1, cols), jnp.float32),
            pltpu.SemaphoreType.DMA((2 * pl.cdiv(rows, min(64, rows)),)),
        ],
        compiler_params=pltpu.CompilerParams(vmem_limit_bytes=20 << 20),
        cost_estimate=pl.CostEstimate(flops=4 * rows * cols, bytes_accessed=16 * rows * cols, transcendentals=0),
        name="finish",
    )(*in_vmem(sums, row_moment[None, :], col_moment, gradient, weight))


def per_device(acts, out_grads, weight, row_state, col_state):
    n_row = lax.axis_size("row")
    n_col = lax.axis_size("col")
    depth = n_row // 4
    width = acts.shape[1]
    tokens = acts.shape[0]
    half, quarter = tokens // 2, tokens // 4
    cols_all = out_grads.shape[1] * n_col
    count_all = width * cols_all
    me = lax.axis_index("row")
    side = lax.axis_index("col") % 2

    def swap(v, bit):
        return lax.ppermute(v, "row", [(i, i ^ bit) for i in range(n_row)])

    def along_z(by, v):
        return lax.ppermute(v, "row", [(i, (i + 4 * by) % n_row) for i in range(n_row)])

    own, pieces = {0: out_grads}, {}
    by_x, by_y = swap(out_grads, 1), swap(out_grads, 2)
    top = swap(by_x[:half], 2)
    pieces[0] = [own[0], by_x, by_y, top, swap(by_y[half:], 1)]
    for k in planes_of(depth):
        by = 1 if 2 * k <= depth else -1
        before = (k - by) % depth
        own[k] = along_z(by, own[before])
        by_x, by_y = swap(own[k], 1), swap(own[k], 2)
        if before == 0:
            far, cut = [along_z(by, top)], half + quarter
            q1, q2 = by_x[half:cut], by_y[cut:]
        else:
            far, q1, q2 = [], by_x[:half], by_y[half:]
        pieces[k] = [own[k], by_x, by_y] + far + [swap(q1, 2), swap(q2, 1)]

    side = side[None]
    blocks = pack(side, acts, n_row)
    blocks = lax.all_to_all(blocks, "row", 0, 0, tiled=True)
    *sooner, last = planes = [0] + planes_of(depth)
    early = [(k, 0) for k in planes] + [(k, j) for k in sooner for j in (1, 2)] + [(0, 3), (last, 1), (last, 2)]
    late = [(k, 3) for k in planes[1:]]
    below = jnp.array([(-k % depth) * 4 for k, _ in early + late], jnp.int32)
    place = jnp.array([j for _, j in early + late], jnp.int32)
    mine = arrange((me - me % 4 + below) % n_row + ((me % 4) ^ place), blocks)
    other = lax.ppermute(mine, "col", [(i, i ^ 1) for i in range(n_col)])
    of = lambda shards: [p for k, j in shards for p in (pieces[k][3:] if j == 3 else [pieces[k][j]])]
    near, far = of(early), of(late)
    gradient, row_squares = last_gemm(side, mine, other, gemm(side, mine, other, near), far)

    row_total = butterfly(row_squares[0], "col", powers(1, n_col))
    row_moment = decay_rate * row_state + (1.0 - decay_rate) * (row_total / cols_all)
    squares = gradient * gradient
    spare = jnp.sum(weight * weight, axis=0)
    spare = jnp.sum(spare.reshape(-1, LANES), axis=0)
    totals = jnp.stack(
        [
            jnp.concatenate([jnp.sum(squares + floor_eps, axis=0), spare]),
            jnp.concatenate([jnp.sum(squares * (1.0 / row_moment)[:, None], axis=0), jnp.zeros_like(spare)]),
        ]
    )
    totals = butterfly(butterfly(totals, "row", [1, 2]), "row", powers(4, n_row))
    col_moment, sums = moments(width, totals, col_state)
    sums = butterfly(sums, "col", powers(1, n_col))
    new_weight, update = finish(count_all, sums, row_moment, col_moment, gradient, weight)
    return (new_weight, update, row_moment, col_moment[0])


def planes_of(depth):
    return [k for i in range(1, depth // 2) for k in (i, depth - i)] + [depth // 2]


def solution(mesh):
    return jax.shard_map(
        per_device,
        mesh=mesh,
        in_specs=(P("row", None), P("row", "col"), P("row", "col"), P("row"), P("col")),
        out_specs=(P("row", "col"), P("row", "col"), P("row"), P("col")),
        check_vma=False,
    )
```

```python
import functools

import jax
import jax.numpy as jnp
from jax import lax
from jax.experimental import pallas as pl
from jax.experimental.pallas import tpu as pltpu
from jax.sharding import PartitionSpec as P

decay_rate = 0.85
floor_eps = 1e-30
relative_rate = 0.05
LANES = 128


def spans(offsets):
    out = [0]
    for offset in offsets:
        out = out + [offset ^ s for s in out]
    return out


def butterfly(value, axis, offsets):
    n = lax.axis_size(axis)
    terms = [value]
    for s in spans(offsets)[1:]:
        terms.append(lax.ppermute(value, axis, [(i, i ^ s) for i in range(n)]))
    while len(terms) > 1:
        terms = [a + b for a, b in zip(terms[::2], terms[1::2])]
    return terms[0]


def powers(first, end):
    out = []
    while first < end:
        out.append(first)
        first *= 2
    return out


def placed(space, arrays):
    return [pltpu.with_memory_space_constraint(a, space) for a in arrays]


def in_vmem(*arrays):
    return placed(pltpu.VMEM, arrays)


WHOLE = pl.BlockSpec(memory_space=pltpu.VMEM)
SCALARS = pl.BlockSpec(memory_space=pltpu.SMEM)


def pack_kernel(side_ref, acts_ref, out_ref):
    _, _, width = out_ref.shape
    low = side_ref[0] == 0
    for d in range(out_ref.shape[0]):
        at = 2 * d * width
        a, b = acts_ref[:, at : at + width], acts_ref[:, at + width : at + 2 * width]
        out_ref[d] = jnp.where(low, a, b)


def pack(side, acts, n_row):
    tokens, width = acts.shape
    return pl.pallas_call(
        pack_kernel,
        out_shape=jax.ShapeDtypeStruct((n_row, tokens, width // (2 * n_row)), acts.dtype),
        in_specs=[SCALARS, WHOLE],
        out_specs=WHOLE,
        compiler_params=pltpu.CompilerParams(vmem_limit_bytes=12 << 20),
        cost_estimate=pl.CostEstimate(flops=0, bytes_accessed=3 * acts.size, transcendentals=0),
        name="pack",
    )(side, acts)


def arrange_kernel(index_ref, blocks_ref, out_ref):
    n_row, tokens, _ = blocks_ref.shape
    for s in range(n_row):
        out_ref[:, s * tokens : (s + 1) * tokens] = blocks_ref[index_ref[s]].T


def arrange(index, blocks):
    n_row, tokens, rows = blocks.shape
    return pl.pallas_call(
        arrange_kernel,
        out_shape=pltpu.VMEM((rows, n_row * tokens), blocks.dtype),
        in_specs=[SCALARS, WHOLE],
        out_specs=WHOLE,
        compiler_params=pltpu.CompilerParams(vmem_limit_bytes=12 << 20),
        cost_estimate=pl.CostEstimate(flops=0, bytes_accessed=8 * blocks.size, transcendentals=0),
        name="arrange",
    )(index, *in_vmem(blocks))


def fill(slab, pieces, lanes):
    at = 0
    for piece in pieces:
        slab[at : at + piece.shape[0], :] = piece[:, lanes]
        at += piece.shape[0]


def gemm_kernel(side_ref, mine_ref, other_ref, *refs):
    *pieces, out_ref, slab, sems = refs
    depth, cols = slab.shape
    height = mine_ref.shape[0]
    width = min(512, cols)
    blocks = [slice(t, t + width) for t in range(0, cols, width)]
    copies = []
    for t, lanes in enumerate(blocks):
        at = 0
        for p, piece in enumerate(pieces):
            here = slice(at, at + piece.shape[0])
            sem = sems.at[t * len(pieces) + p]
            copies.append(pltpu.make_async_copy(piece.at[:, lanes], slab.at[here, lanes], sem))
            copies[-1].start()
            at += piece.shape[0]
    for t, lanes in enumerate(blocks):
        for copy in copies[t * len(pieces) : (t + 1) * len(pieces)]:
            copy.wait()
        for at, columns_ref in ((side_ref[0], mine_ref), (1 - side_ref[0], other_ref)):
            rows = pl.ds(pl.multiple_of(at * height, height), height)
            out_ref[rows, lanes] = jnp.dot(columns_ref[:, :depth], slab[:, lanes], preferred_element_type=jnp.float32)


def gemm(side, mine, other, pieces):
    rows = 2 * mine.shape[0]
    depth = sum(p.shape[0] for p in pieces)
    cols = pieces[0].shape[1]
    return pl.pallas_call(
        gemm_kernel,
        out_shape=pltpu.VMEM((rows, cols), jnp.float32),
        in_specs=[SCALARS, WHOLE, WHOLE] + [pl.BlockSpec(memory_space=pl.ANY)] * (len(pieces) - 2) + [WHOLE] * 2,
        out_specs=WHOLE,
        scratch_shapes=[
            pltpu.VMEM((depth, cols), jnp.bfloat16),
            pltpu.SemaphoreType.DMA((len(pieces) * pl.cdiv(cols, 512),)),
        ],
        compiler_params=pltpu.CompilerParams(vmem_limit_bytes=24 << 20),
        cost_estimate=pl.CostEstimate(flops=2 * rows * depth * cols, bytes_accessed=2 * depth * cols, transcendentals=0),
        name="gemm",
    )(side, *in_vmem(mine, other), *placed(pltpu.HBM, pieces[:-2]), *in_vmem(*pieces[-2:]))


def last_kernel(side_ref, mine_ref, other_ref, before_ref, *refs):
    *pieces, out_ref, rows_ref, slab, sums = refs
    depth, width = slab.shape
    height = mine_ref.shape[0]
    first = mine_ref.shape[1] - depth
    cols = out_ref.shape[1]
    side = side_ref[0]
    for t in range(0, cols, width):
        lanes = slice(t, t + width)
        fill(slab, pieces, lanes)
        for at, columns_ref in ((side, mine_ref), (1 - side, other_ref)):
            rows = pl.ds(pl.multiple_of(at * height, height), height)
            total = before_ref[rows, lanes] + jnp.dot(
                columns_ref[:, first:], slab[...], preferred_element_type=jnp.float32
            )
            out_ref[rows, lanes] = total
            squares = total * total + floor_eps
            part = squares[:, :LANES]
            for u in range(LANES, width, LANES):
                part = part + squares[:, u : u + LANES]
            sums[rows, :] = part if t == 0 else sums[rows, :] + part
    rows_ref[...] = jnp.sum(sums[...].T, axis=0, keepdims=True)


def last_gemm(side, mine, other, before, pieces):
    rows, cols = before.shape
    depth = sum(p.shape[0] for p in pieces)
    return pl.pallas_call(
        last_kernel,
        out_shape=[pltpu.VMEM((rows, cols), jnp.float32), pltpu.VMEM((1, rows), jnp.float32)],
        in_specs=[SCALARS] + [WHOLE] * (3 + len(pieces)),
        out_specs=[WHOLE, WHOLE],
        scratch_shapes=[pltpu.VMEM((depth, min(512, cols)), jnp.bfloat16), pltpu.VMEM((rows, LANES), jnp.float32)],
        compiler_params=pltpu.CompilerParams(vmem_limit_bytes=24 << 20),
        cost_estimate=pl.CostEstimate(flops=2 * rows * depth * cols, bytes_accessed=2 * depth * cols, transcendentals=0),
        name="last_gemm",
    )(side, *in_vmem(mine, other, before), *pieces)


def moments_kernel(height, totals_ref, state_ref, col_ref, sums_ref):
    cols = state_ref.shape[1]
    col = decay_rate * state_ref[...] + (1.0 - decay_rate) * (totals_ref[0:1, :cols] / height)
    col_ref[...] = col
    clip = jnp.sum(totals_ref[1:2, :cols] / col)
    weight = jnp.sum(totals_ref[0:1, cols:])
    row = lax.broadcasted_iota(jnp.int32, sums_ref.shape, 0)
    sums_ref[...] = jnp.where(row == 0, clip, weight)


def moments(height, totals, col_state):
    cols = col_state.shape[0]
    whole = pl.BlockSpec(memory_space=pltpu.VMEM)
    return pl.pallas_call(
        functools.partial(moments_kernel, height),
        out_shape=[pltpu.VMEM((1, cols), jnp.float32), pltpu.VMEM((8, LANES), jnp.float32)],
        in_specs=[whole, whole],
        out_specs=[whole, whole],
        compiler_params=pltpu.CompilerParams(vmem_limit_bytes=8 << 20),
        name="moments",
    )(totals, col_state[None, :])


def finish_kernel(count_all, sums_ref, row_ref, col_ref, gradient_ref, weight_ref, new_hbm, update_hbm, new, update, rows, cols, sems):
    clip = jnp.maximum(1.0, jnp.sqrt(sums_ref[0:1, :] / count_all))
    step_size = relative_rate * jnp.sqrt(sums_ref[1:2, :] / count_all + 1e-06)
    root = lax.rsqrt(row_ref[...])
    rows[...] = jnp.broadcast_to(root, (LANES, root.shape[1])).T
    for t in range(0, cols.shape[1], LANES):
        cols[:, t : t + LANES] = lax.rsqrt(col_ref[:, t : t + LANES]) / clip
    height = min(64, rows.shape[0])
    bounds = [0, height // 4] + list(range(height, rows.shape[0] + 1, height))
    copies = []
    for i, here in enumerate(slice(a, b) for a, b in zip(bounds, bounds[1:])):
        scale = rows[here, :]
        for t in range(0, cols.shape[1], LANES):
            lanes = slice(t, t + LANES)
            value = gradient_ref[here, lanes] * scale * cols[:, lanes]
            update[here, lanes] = value
            new[here, lanes] = weight_ref[here, lanes] - step_size * value
        for j, (source, target) in enumerate(((update, update_hbm), (new, new_hbm))):
            copies.append(pltpu.make_async_copy(source.at[here], target.at[here], sems.at[2 * i + j]))
            copies[-1].start()
    for copy in copies:
        copy.wait()


def finish(count_all, sums, row_moment, col_moment, gradient, weight):
    rows, cols = gradient.shape
    out = pltpu.HBM((rows, cols), jnp.float32)
    there = pl.BlockSpec(memory_space=pl.ANY)
    return pl.pallas_call(
        functools.partial(finish_kernel, count_all),
        out_shape=[out, out],
        in_specs=[WHOLE] * 5,
        out_specs=[there, there],
        scratch_shapes=[
            pltpu.VMEM((rows, cols), jnp.float32),
            pltpu.VMEM((rows, cols), jnp.float32),
            pltpu.VMEM((rows, LANES), jnp.float32),
            pltpu.VMEM((1, cols), jnp.float32),
            pltpu.SemaphoreType.DMA((2 * pl.cdiv(rows, min(64, rows)) + 2,)),
        ],
        compiler_params=pltpu.CompilerParams(vmem_limit_bytes=20 << 20),
        cost_estimate=pl.CostEstimate(flops=4 * rows * cols, bytes_accessed=16 * rows * cols, transcendentals=0),
        name="finish",
    )(*in_vmem(sums, row_moment[None, :], col_moment, gradient, weight))


def per_device(acts, out_grads, weight, row_state, col_state):
    n_row = lax.axis_size("row")
    n_col = lax.axis_size("col")
    depth = n_row // 4
    width = acts.shape[1]
    tokens = acts.shape[0]
    half, quarter = tokens // 2, tokens // 4
    cols_all = out_grads.shape[1] * n_col
    count_all = width * cols_all
    me = lax.axis_index("row")
    side = lax.axis_index("col") % 2

    def swap(v, bit):
        return lax.ppermute(v, "row", [(i, i ^ bit) for i in range(n_row)])

    def along_z(by, v):
        return lax.ppermute(v, "row", [(i, (i + 4 * by) % n_row) for i in range(n_row)])

    own, pieces = {0: out_grads}, {}
    by_x, by_y = swap(out_grads, 1), swap(out_grads, 2)
    top = swap(by_x[:half], 2)
    pieces[0] = [own[0], by_x, by_y, top, swap(by_y[half:], 1)]
    for k in planes_of(depth):
        by = 1 if 2 * k <= depth else -1
        before = (k - by) % depth
        own[k] = along_z(by, own[before])
        by_x, by_y = swap(own[k], 1), swap(own[k], 2)
        if before == 0:
            far, cut = [along_z(by, top)], half + quarter
            q1, q2 = by_x[half:cut], by_y[cut:]
        else:
            far, q1, q2 = [], by_x[:half], by_y[half:]
        pieces[k] = [own[k], by_x, by_y] + far + [swap(q1, 2), swap(q2, 1)]

    side = side[None]
    blocks = pack(side, acts, n_row)
    blocks = lax.all_to_all(blocks, "row", 0, 0, tiled=True)
    *sooner, last = planes = [0] + planes_of(depth)
    early = [(k, 0) for k in planes] + [(k, j) for k in sooner for j in (1, 2)] + [(0, 3), (last, 1), (last, 2)]
    late = [(k, 3) for k in planes[1:]]
    below = jnp.array([(-k % depth) * 4 for k, _ in early + late], jnp.int32)
    place = jnp.array([j for _, j in early + late], jnp.int32)
    mine = arrange((me - me % 4 + below) % n_row + ((me % 4) ^ place), blocks)
    other = lax.ppermute(mine, "col", [(i, i ^ 1) for i in range(n_col)])
    of = lambda shards: [p for k, j in shards for p in (pieces[k][3:] if j == 3 else [pieces[k][j]])]
    near, far = of(early), of(late)
    gradient, row_squares = last_gemm(side, mine, other, gemm(side, mine, other, near), far)

    row_total = butterfly(row_squares[0], "col", powers(1, n_col))
    row_moment = decay_rate * row_state + (1.0 - decay_rate) * (row_total / cols_all)
    squares = gradient * gradient
    spare = jnp.sum(weight * weight, axis=0)
    spare = jnp.sum(spare.reshape(-1, LANES), axis=0)
    totals = jnp.stack(
        [
            jnp.concatenate([jnp.sum(squares + floor_eps, axis=0), spare]),
            jnp.concatenate([jnp.sum(squares * (1.0 / row_moment)[:, None], axis=0), jnp.zeros_like(spare)]),
        ]
    )
    totals = butterfly(butterfly(totals, "row", [1, 2]), "row", powers(4, n_row))
    col_moment, sums = moments(width, totals, col_state)
    sums = butterfly(sums, "col", powers(1, n_col))
    new_weight, update = finish(count_all, sums, row_moment, col_moment, gradient, weight)
    return (new_weight, update, row_moment, col_moment[0])


def planes_of(depth):
    return [k for i in range(1, depth // 2) for k in (i, depth - i)] + [depth // 2]


def solution(mesh):
    return jax.shard_map(
        per_device,
        mesh=mesh,
        in_specs=(P("row", None), P("row", "col"), P("row", "col"), P("row"), P("col")),
        out_specs=(P("row", "col"), P("row", "col"), P("row"), P("col")),
        check_vma=False,
    )
```
